256 devices in a mesh: samp: 64 (over z, x, y_lo), snp: 4 (over y_hi, core).
Axes of the slice: x: 4, y: 4 (y_hi: 2, y_lo: 2; y = y_hi * 2 + y_lo), z: 8, core: 2. Of those that a mesh axis runs over, the one named last changes fastest.
Arguments:
- genotypes: bfloat16 [32768, 16384], P('samp', 'snp'), may hold values from 0 to 2, as said below
- traits: bfloat16 [32768, 256], P('samp'), may hold values from -40 to 40
- trait_basis: float32 [256, 64], replicated, may hold values from -0.375 to 0.375
Outputs:
- fitted: bfloat16 [32768, 256], P('samp')
- covariance: float32 [256, 256], replicated
- scores: float32 [32768, 64], P('samp')
The draws below stay inside these ranges and needn't reach their ends.
Inputs may be any that keep to these rules, and one draw needn't show every extreme that they name: `genotypes`: every entry is a whole number of alleles: 0, 1 or 2.
All inputs are finite; a program needn't handle non-finite values.
Results may differ from the reference program's by a relative error of at most 0.0044.
Values may be sent and summed in bfloat16 or wider, within the bound.
A program may use at most 64 MiB of HBM per device.

```python
import math
import jax
import jax.numpy as jnp
from jax import lax

P_SIZE = 16384
K = 256
RANK = 64
NS = 32768
N_SNP = 4


def draw_genotypes(key, part):
    rate_key, allele_key = jax.random.split(key)
    slice_width = P_SIZE // N_SNP
    position = jnp.arange(P_SIZE, dtype=jnp.int32)[None, :] % slice_width
    rising = 8 + 52 * position // slice_width
    jitter = jax.random.randint(rate_key, (1, P_SIZE), 0, 5)
    allele_rate = rising + jitter
    uniform_draw = jax.random.randint(allele_key, (NS, P_SIZE), 0, 400)
    dosage = (uniform_draw < allele_rate).astype(jnp.int32) + (uniform_draw < allele_rate // 4).astype(jnp.int32)
    return dosage.astype(jnp.float32).astype(jnp.bfloat16)


def draw_traits(key, part):
    scale_key = jax.random.fold_in(key, 0)
    row_key = jax.random.fold_in(key, 1)
    noise_key = jax.random.fold_in(key, 2)
    level_key = jax.random.fold_in(key, 4)
    row_index = jnp.arange(NS, dtype=jnp.float32)[:, None]
    col_scale = jnp.exp(jax.random.uniform(scale_key, (1, K), minval=math.log(0.5), maxval=math.log(3.0)))
    col_level = jnp.exp(jax.random.uniform(level_key, (1, K), minval=math.log(0.5), maxval=math.log(2.5)))
    row_scale = (0.5 + 1.5 * row_index / NS) * jnp.exp(jax.random.uniform(row_key, (NS, 1), minval=math.log(0.7), maxval=math.log(1.4)))
    noise_field = jax.random.truncated_normal(noise_key, -3.0, 3.0, (NS, K))
    return (col_level + noise_field * col_scale * row_scale).astype(jnp.float32).astype(jnp.bfloat16)


def bell_draw(stream_key, extent, deviation, bound, kind=jnp.bfloat16):
    entries = deviation * jax.random.normal(stream_key, extent, jnp.float32)
    return jnp.clip(entries, min=-bound, max=bound).astype(kind)


def setup_inputs(seed: int = 0) -> dict:
    streams_of = jax.random.split(jax.random.key(seed), 4)
    return {
        "genotypes": draw_genotypes(jax.random.fold_in(streams_of[3], 71), 0),
        "traits": draw_traits(jax.random.fold_in(streams_of[3], 71), 0),
        "trait_basis": bell_draw(streams_of[2], (K, RANK), K ** -0.5, 0.375, jnp.float32),
    }


def reference(genotypes, traits, trait_basis):
    highest = lax.Precision.HIGHEST
    geno_mean = jnp.sum(genotypes, axis=0, dtype=jnp.float32) / NS
    trait_sums = jnp.sum(traits, axis=0, dtype=jnp.float32)
    normal = lax.dot_general(genotypes, traits, (((0,), (0,)), ((), ())), preferred_element_type=jnp.float32)
    normal = normal - geno_mean[:, None] * trait_sums[None, :]
    norm_sq = jnp.sum(normal * normal, axis=0)
    normal_bf = normal.astype(jnp.bfloat16)
    shifted = jnp.dot(geno_mean, normal_bf.astype(jnp.float32), precision=highest)
    projected = jnp.dot(genotypes, normal_bf, preferred_element_type=jnp.float32) - shifted[None, :]
    gram_raw = lax.dot_general(projected, projected, (((0,), (0,)), ((), ())), precision=highest)
    step_size = norm_sq / (jnp.diagonal(gram_raw) + (NS / 8.0) * norm_sq)
    fitted = (projected * step_size[None, :]).astype(jnp.bfloat16)
    covariance = step_size[:, None] * gram_raw * step_size[None, :] / NS
    loading = jnp.dot(covariance, trait_basis, precision=highest)
    spread = jnp.trace(covariance) + 1e-6
    scores = K * jnp.dot(fitted.astype(jnp.float32), loading, precision=highest) / spread
    return fitted, covariance, scores
```

```python
import functools

import jax
import jax.numpy as jnp
from jax import lax
from jax.experimental import pallas as pl
from jax.experimental.pallas import tpu as pltpu
from jax.sharding import PartitionSpec as P

MESH = pl.DeviceIdType.MESH
F32, BF16 = jnp.float32, jnp.bfloat16
HIGHEST = lax.Precision.HIGHEST
SIZE = {"x": 4, "y": 2, "z": 8}
ROWS, SNPS, TRAITS, RANK = 512, 4096, 256, 64
SAMPLES = 64 * ROWS
PARTS = ((("x", "z", "y"), 0, 32), (("y", "x", "z"), 2048, 32))


def rows_of(part):
    return part[2] * 64


def kernel(g_hbm, t_hbm, basis_ref, fit_ref, cov_ref, score_ref, *scratch):
    it = iter(scratch)
    g, t, raw, gsum = next(it), next(it), next(it), next(it)
    tsum, tsum_in, tile, tile_in, mean_all, norm_in = (next(it) for _ in range(6))
    parts = [tuple(next(it) for _ in range(8)) for _ in PARTS]
    p, pb, pb_in, half, hb, hb_in, full = (next(it) for _ in range(7))
    gt, gt_in, gz_in, gx_in, gy_in, gall = (next(it) for _ in range(6))
    load_sem, send_sem, recv_sem = next(it), next(it), next(it)

    samp, snp = lax.axis_index("samp"), lax.axis_index("snp")
    me = {"x": lax.rem(samp // 2, 4), "y": lax.rem(samp, 2), "z": samp // 8}
    yh, core = snp // 2, lax.rem(snp, 2)

    def at(dim, k):
        n = SIZE[dim]
        to = lax.rem(me[dim] + k, n)
        c = dict(me)
        c[dim] = to
        return to, ((c["z"] * 4 + c["x"]) * 2 + c["y"], snp)

    other_core = (samp, yh * 2 + (1 - core))
    other_half = (samp, (1 - yh) * 2 + core)
    y_peer = at("y", 1)[1]
    y_far = (y_peer[0], other_half[1])

    peers = [at(d, k)[1] for d in "xyz" for k in range(1, SIZE[d])]
    peers += [other_core, other_half, y_far]
    barrier = pltpu.get_barrier_semaphore()
    for dev in peers:
        pl.semaphore_signal(barrier, inc=1, device_id=dev, device_id_type=MESH)

    t_copy = pltpu.make_async_copy(t_hbm, t, load_sem.at[4])
    t_copy.start()
    g_copies = []
    for i in range(4):
        cols = pl.ds(i * 1024, 1024)
        cp = pltpu.make_async_copy(g_hbm.at[:, cols], g.at[:, cols], load_sem.at[i])
        cp.start()
        g_copies.append(cp)

    count = [0]
    started = []

    def send(src, dst, dev):
        i = count[0]
        count[0] += 1
        cp = pltpu.make_async_remote_copy(
            src_ref=src, dst_ref=dst, send_sem=send_sem.at[i], recv_sem=recv_sem.at[i],
            device_id=dev, device_id_type=MESH)
        cp.start()
        started.append(cp)
        return cp

    def wait(copies):
        for cp in copies:
            cp.wait_recv()

    t_copy.wait()

    def add_rows(i, acc):
        b = t[pl.ds(pl.multiple_of(i * 64, 64), 64), :].astype(F32)
        return acc + jnp.sum(b.reshape(8, 8, TRAITS), axis=0)

    acc = lax.fori_loop(0, ROWS // 64, add_rows, jnp.zeros((8, TRAITS), F32))
    tot = jnp.sum(acc, axis=0, keepdims=True)
    tsum[0] = jnp.concatenate([tot] * 8, axis=0)
    pl.semaphore_wait(barrier, len(peers))

    ones = jnp.ones((ROWS, 128), BF16)

    def product(i):
        cols = pl.ds(i * 512, 512)
        blk = g[:, cols]
        dims = (((0,), (0,)), ((), ()))
        raw[cols, :] = lax.dot_general(blk, t[...], dims, preferred_element_type=F32)
        gsum[cols, :] = lax.dot_general(blk, ones, dims, preferred_element_type=F32)

    slot = 0
    blocks = [[0, 1, 2], [3, 4, 5], [6, 7]]
    for s, d in enumerate("xzy"):
        n = SIZE[d]
        cps = [send(tsum.at[s], tsum_in.at[slot + k - 1], at(d, k)[1]) for k in range(1, n)]
        for i in blocks[s]:
            if i % 2 == 0:
                g_copies[i // 2].wait()
            product(i)
        wait(cps)
        v = tsum[s]
        for k in range(n - 1):
            v = v + tsum_in[slot + k]
        tsum[s + 1] = v
        slot += n - 1

    def centred(r0, n):
        rows = pl.ds(r0, n)
        c = tsum[3] * (1.0 / SAMPLES)
        c = jnp.concatenate([c] * (n // 8), axis=0)
        s = gsum[rows, :]
        return raw[rows, :] - jnp.concatenate([s, s], axis=1) * c

    def stage_one(part, bufs):
        order, first, own = part
        d = order[0]
        n = SIZE[d]
        blk = rows_of(part) // n
        out, inn = bufs[0], bufs[1]
        cps = []
        for k in range(1, n):
            to, dev = at(d, k)

            def fill(i, _):
                r = pl.multiple_of(i * 32, 32)
                out[k - 1, pl.ds(r, 32), :] = centred(pl.multiple_of(first + to * blk + r, 32), 32).astype(BF16)
                return 0

            lax.fori_loop(0, blk // 32, fill, 0)
            cps.append(send(out.at[k - 1], inn.at[k - 1], dev))
        return cps

    def sum_one(part, bufs):
        order, first, own = part
        n = SIZE[order[0]]
        blk = rows_of(part) // n
        inn, two = bufs[1], bufs[2]
        mine = me[order[0]]
        sub = blk // SIZE[order[1]]

        def body(i, _):
            r = pl.multiple_of(i * 32, 32)
            v = centred(pl.multiple_of(first + mine * blk + r, 32), 32)
            for k in range(n - 1):
                v = v + inn[k, pl.ds(r, 32), :].astype(F32)
            two[pl.ds(r, 32), :] = v.astype(BF16)

            @pl.when(r // sub == me[order[1]])
            def _():
                bufs[7][pl.ds(pl.multiple_of(lax.rem(r, sub), 32), 32), :] = v
            return 0

        lax.fori_loop(0, blk // 32, body, 0)

    def stage_two(part, bufs):
        order, first, own = part
        d = order[1]
        sub = own * SIZE[order[2]]
        cps = []
        for k in range(1, SIZE[d]):
            to, dev = at(d, k)
            cps.append(send(bufs[2].at[pl.ds(pl.multiple_of(to * sub, 32), sub), :], bufs[3].at[k - 1], dev))
        return cps

    def sum_two(part, bufs):
        order, first, own = part
        n = SIZE[order[1]]
        sub = own * SIZE[order[2]]

        def body(i, _):
            r = pl.multiple_of(i * 32, 32)
            v = bufs[7][pl.ds(r, 32), :]
            for k in range(n - 1):
                v = v + bufs[3][k, pl.ds(r, 32), :].astype(F32)
            bufs[7][pl.ds(r, 32), :] = v
            bufs[4][pl.ds(r, 32), :] = v.astype(BF16)
            return 0

        lax.fori_loop(0, sub // 32, body, 0)

    def stage_three(part, bufs):
        order, first, own = part
        d = order[2]
        cps = []
        for k in range(1, SIZE[d]):
            to, dev = at(d, k)
            cps.append(send(bufs[4].at[pl.ds(pl.multiple_of(to * own, 16), own), :], bufs[5].at[k - 1], dev))
        return cps

    def where(part):
        order = part[0]
        return tuple(me[d] for d in order)

    def sum_three(part, bufs):
        order, first, own = part
        n = SIZE[order[2]]
        v = bufs[7][pl.ds(pl.multiple_of(me[order[2]] * own, 16), own), :]
        for k in range(n - 1):
            v = v + bufs[5][k].astype(F32)
        a, b, c = where(part)
        bufs[6][a, b, c] = v.astype(BF16)
        return jnp.sum(v * v, axis=0, keepdims=True)

    both = list(zip(PARTS, parts))
    one = [stage_one(*pb_) for pb_ in both]
    two, three = [], []
    for pb_, cps in zip(both, one):
        wait(cps)
        sum_one(*pb_)
        two.append(stage_two(*pb_))
    for pb_, cps in zip(both, two):
        wait(cps)
        sum_two(*pb_)
        three.append(stage_three(*pb_))
    norm = jnp.zeros((1, TRAITS), F32)
    gather = []
    for (part, bufs), cps in zip(both, three):
        wait(cps)
        norm = norm + sum_three(part, bufs)
        a, b, c = where(part)
        piece = bufs[6].at[a, b, c]
        gather.append([send(piece, piece, at(part[0][2], k)[1]) for k in range(1, SIZE[part[0][2]])])
    norm8 = jnp.concatenate([norm[:, :128], norm[:, 128:]] + [jnp.zeros((6, 128), F32)], axis=0)
    tile[0] = norm8

    def norm_step(s, d, slot):
        n = SIZE[d]
        return [send(tile.at[s], norm_in.at[slot + k - 1], at(d, k)[1]) for k in range(1, n)]

    def norm_sum(s, d, slot):
        v = tile[s]
        for k in range(SIZE[d] - 1):
            v = v + norm_in[slot + k]
        tile[s + 1] = v

    nx = norm_step(0, "x", 0)
    gather2 = []
    for (part, bufs), cps in zip(both, gather):
        wait(cps)
        a, b, c = where(part)
        piece = bufs[6].at[a, b]
        gather2.append([send(piece, piece, at(part[0][1], k)[1]) for k in range(1, SIZE[part[0][1]])])
    wait(nx)
    norm_sum(0, "x", 0)
    nz = norm_step(1, "z", 3)
    gather3 = []
    for (part, bufs), cps in zip(both, gather2):
        wait(cps)
        a, b, c = where(part)
        piece = bufs[6].at[a]
        gather3.append([send(piece, piece, at(part[0][0], k)[1]) for k in range(1, SIZE[part[0][0]])])
    wait(nz)
    norm_sum(1, "z", 3)
    ny = norm_step(2, "y", 10)

    def project(part, bufs, a, start):
        order, first, own = part
        blk = rows_of(part) // SIZE[order[0]]
        cols = pl.ds(pl.multiple_of(first + a * blk, 128), blk)
        v = jnp.dot(g[:, cols], bufs[6][a].reshape(blk, TRAITS), preferred_element_type=F32)
        if start:
            p[...] = v
        else:
            p[...] += v

    for i, (part, bufs) in enumerate(both):
        project(part, bufs, me[part[0][0]], i == 0)
    wait(ny)
    norm_sum(2, "y", 10)
    for (part, bufs), cps in zip(both, gather3):
        d = part[0][0]
        for k, cp in enumerate(cps):
            cp.wait_recv()
            project(part, bufs, lax.rem(me[d] + SIZE[d] - (k + 1), SIZE[d]), False)

    mean = jnp.sum(p[...], axis=0, keepdims=True) * (1.0 / ROWS)
    tile[4] = jnp.concatenate([mean[:, :128], mean[:, 128:], tile[3][:2], jnp.zeros((4, 128), F32)], axis=0)
    away = pl.multiple_of((1 - core) * 256, 256)
    pb[...] = p[pl.ds(away, 256), :] - mean
    c1 = [send(pb, pb_in, other_core), send(tile.at[4], tile_in.at[0], other_core)]
    wait(c1)
    tile[5] = tile[4] + tile_in[0]
    half[...] = p[pl.ds(pl.multiple_of(core * 256, 256), 256), :] - mean + pb_in[...]
    hb[...] = half[pl.ds(pl.multiple_of((1 - yh) * 128, 128), 128), :]
    c2 = [send(hb, hb_in, other_half), send(tile.at[5], tile_in.at[1], other_half)]
    wait(c2)
    tile[6] = tile[5] + tile_in[1]
    mine = half[pl.ds(pl.multiple_of(yh * 128, 128), 128), :] + hb_in[...]
    full[core, yh] = mine
    c3 = [send(full.at[core, yh], full.at[core, yh], other_half)]

    mean_all[me["z"], me["x"], me["y"]] = tile[6]
    piece = mean_all.at[me["z"], me["x"], me["y"]]
    m1 = [send(piece, piece, at("x", k)[1]) for k in range(1, 4)]

    dims0 = (((0,), (0,)), ((), ()))
    a_gram = lax.dot_general(mine, mine, dims0, precision=HIGHEST, preferred_element_type=F32)
    for r in range(32):
        for c in range(2):
            gt[r // 16, (r // 2) % 8, (r % 2) * 2 + c] = a_gram[r * 8:r * 8 + 8, c * 128:c * 128 + 128]
    g1 = [send(gt.at[1 - core], gt_in, other_core)]
    wait(g1)
    for z in range(8):
        gt_in[z] = gt_in[z] + gt[core, z]
    g2 = []
    for k in range(1, 8):
        to, dev = at("z", k)
        g2.append(send(gt_in.at[to], gz_in.at[k - 1], dev))
    wait(m1)
    piece = mean_all.at[me["z"], :, me["y"]]
    m2 = []
    for x in range(4):
        piece = mean_all.at[me["z"], x, me["y"]]
        m2 += [send(piece, piece, at("z", k)[1]) for k in range(1, 8)]
    wait(g2)
    v = gt_in[me["z"]]
    for k in range(7):
        v = v + gz_in[k]
    gz_in[7] = v
    g3 = []
    for k in range(1, 4):
        to, dev = at("x", k)
        g3.append(send(gz_in.at[7, to], gx_in.at[k - 1], dev))
    wait(c3)
    c4 = [send(full.at[core], full.at[core], other_core)]
    wait(g3)
    v = gz_in[7, me["x"]]
    for k in range(3):
        v = v + gx_in[k]
    gy_in[3] = v
    g4 = [send(gy_in.at[3], gy_in.at[i], dev) for i, dev in enumerate((y_peer, other_half, y_far))]
    wait(g4)
    gall[core, me["z"], me["x"]] = gy_in[3] + gy_in[0] + (gy_in[1] + gy_in[2])
    piece = gall.at[core, me["z"], me["x"]]
    g5 = [send(piece, piece, at("x", k)[1]) for k in range(1, 4)]
    wait(m2)
    m3 = []
    for z in range(8):
        for x in range(4):
            piece = mean_all.at[z, x, me["y"]]
            m3.append(send(piece, piece, y_peer))
    wait(g5)
    piece = gall.at[core, me["z"]]
    g6 = [send(piece, piece, at("z", k)[1]) for k in range(1, 8)]
    wait(g6)
    piece = gall.at[core]
    g7 = [send(piece, piece, other_core)]
    wait(m3)
    wait(c4)
    means = jnp.concatenate([mean_all[z, x, y] for z in range(8) for x in range(4) for y in range(2)], axis=0)
    means = means.reshape(64, 8, 128)
    means = jnp.concatenate([means[:, 0, :], means[:, 1, :]], axis=1)
    centre = jnp.sum(means, axis=0, keepdims=True) * (1.0 / 64)
    dev_ = means - centre
    between = lax.dot_general(dev_, dev_, dims0, precision=HIGHEST, preferred_element_type=F32) * float(ROWS)
    norm_row = jnp.concatenate([tile[6][2:3], tile[6][3:4]], axis=1)
    off = jnp.concatenate([tile[6][0:1], tile[6][1:2]], axis=1) - centre
    wait(g7)
    rows = []
    for r in range(32):
        rows.append(jnp.concatenate(
            [gall[r // 16, (r // 2) % 8, (r % 2) * 2 + c] for c in range(2)], axis=1))
    gram = jnp.concatenate(rows, axis=0) + between
    eye = (lax.broadcasted_iota(jnp.int32, (TRAITS, TRAITS), 0)
           == lax.broadcasted_iota(jnp.int32, (TRAITS, TRAITS), 1))
    diag = jnp.where(eye, gram, 0.0)
    diag_row = jnp.sum(diag, axis=0, keepdims=True)
    step_row = norm_row / (diag_row + (SAMPLES / 8.0) * norm_row)
    step_col = jnp.sum(jnp.where(eye, jnp.broadcast_to(step_row, (TRAITS, TRAITS)), 0.0), axis=1, keepdims=True)
    cov = step_col * gram * step_row * (1.0 / SAMPLES)
    cov_ref[...] = cov
    spread = jnp.sum(step_row * step_row * diag_row, axis=1, keepdims=True) * (1.0 / SAMPLES) + 1e-6
    loading = jnp.dot(cov, basis_ref[...], precision=HIGHEST, preferred_element_type=F32) * (TRAITS / spread)
    high = loading.astype(BF16)
    low = (loading - high.astype(F32)).astype(BF16)
    for c in range(2):
        for h in range(2):
            r = pl.ds((c * 2 + h) * 128, 128)
            f = ((full[c, h] + off) * step_row).astype(BF16)
            fit_ref[r, :] = f
            score_ref[r, :] = (jnp.dot(f, high, preferred_element_type=F32)
                               + jnp.dot(f, low, preferred_element_type=F32))
    for cp in started:
        cp.wait_send()
    assert count[0] == COPIES, count[0]


COPIES = 160


def scratch_of():
    vmem = pltpu.VMEM
    shapes = [
        vmem((ROWS, SNPS), BF16), vmem((ROWS, TRAITS), BF16), vmem((SNPS, TRAITS), F32), vmem((SNPS, 128), F32),
        vmem((4, 8, TRAITS), F32), vmem((11, 8, TRAITS), F32),
        vmem((7, 8, 128), F32), vmem((2, 8, 128), F32), vmem((8, 4, 2, 8, 128), F32), vmem((11, 8, 128), F32),
    ]
    for part in PARTS:
        order, first, own = part
        n1, n2, n3 = (SIZE[d] for d in order)
        rows = rows_of(part)
        shapes += [
            vmem((n1 - 1, rows // n1, TRAITS), BF16), vmem((n1 - 1, rows // n1, TRAITS), BF16),
            vmem((rows // n1, TRAITS), BF16), vmem((n2 - 1, own * n3, TRAITS), BF16),
            vmem((own * n3, TRAITS), BF16), vmem((n3 - 1, own, TRAITS), BF16),
            vmem((n1, n2, n3, own, TRAITS), BF16), vmem((own * n3, TRAITS), F32),
        ]
    shapes += [
        vmem((ROWS, TRAITS), F32), vmem((256, TRAITS), F32), vmem((256, TRAITS), F32), vmem((256, TRAITS), F32),
        vmem((128, TRAITS), F32), vmem((128, TRAITS), F32), vmem((2, 2, 128, TRAITS), F32),
        vmem((2, 8, 4, 8, 128), F32), vmem((8, 4, 8, 128), F32), vmem((8, 4, 8, 128), F32), vmem((3, 8, 128), F32),
        vmem((4, 8, 128), F32), vmem((2, 8, 4, 8, 128), F32),
        pltpu.SemaphoreType.DMA((5,)), pltpu.SemaphoreType.DMA((COPIES,)), pltpu.SemaphoreType.DMA((COPIES,)),
    ]
    return shapes


def local(genotypes, traits, trait_basis):
    anywhere = pl.BlockSpec(memory_space=pl.ANY)
    inside = pl.BlockSpec(memory_space=pltpu.VMEM)
    return pl.pallas_call(
        kernel,
        out_shape=(
            jax.ShapeDtypeStruct((ROWS, TRAITS), BF16),
            jax.ShapeDtypeStruct((TRAITS, TRAITS), F32),
            jax.ShapeDtypeStruct((ROWS, RANK), F32),
        ),
        in_specs=[anywhere, anywhere, inside],
        out_specs=(inside, inside, inside),
        scratch_shapes=scratch_of(),
        compiler_params=pltpu.CompilerParams(
            collective_id=0, has_side_effects=True, vmem_limit_bytes=56 * 2**20),
    )(genotypes, traits, trait_basis)


def solution(mesh):
    return jax.shard_map(
        local,
        mesh=mesh,
        in_specs=(P("samp", "snp"), P("samp", None), P()),
        out_specs=(P("samp", None), P(), P("samp", None)),
        check_vma=False,
    )
```

```python
import itertools

import jax
import jax.numpy as jnp
from jax import lax
from jax.experimental import pallas as pl
from jax.experimental.pallas import tpu as pltpu
from jax.sharding import PartitionSpec as P

MESH = pl.DeviceIdType.MESH
F32, BF16 = jnp.float32, jnp.bfloat16
HIGHEST = lax.Precision.HIGHEST
SIZE = {"x": 4, "y": 2, "z": 8, "h": 2}
ROWS, SNPS, TRAITS, RANK = 512, 4096, 256, 64
GROUPS = 64
SAMPLES = GROUPS * ROWS
DIMS0 = (((0,), (0,)), ((), ()))
PLANE, ALONG = ("x", "y"), ("z",)
PARTS = ((PLANE, ALONG), (ALONG, PLANE), (PLANE, ALONG), (PLANE, ALONG))
PART = SNPS // len(PARTS)
OWN = PART // GROUPS
ORDER = [(0, 0), (1, 0), (2, 0), (3, 0), (0, 1), (2, 1), (1, 1), (0, 2), (3, 1), (2, 2), (1, 2), (0, 3), (3, 2), (2, 3),
         (1, 3), (3, 3), (0, 4), (2, 4), (1, 4), (3, 4)]


SLOTS = {PLANE: (0, 1, 2, 3, 4, 5, 6), ("x",): (1, 3, 5), ("y",): (0,)}


def size_of(group):
    n = 1
    for d in group:
        n *= SIZE[d]
    return n


def steps_of(part):
    return 2 * len(part) + 1


def order_of():
    if ORDER is not None:
        return ORDER
    first = [(i, 0) for i in range(len(PARTS))]
    return first + [(i, t - i) for t in range(16) for i in range(len(PARTS)) if 0 < t - i < steps_of(PARTS[i])]


def dot_rows(a, b):
    return lax.dot_general(a, b, DIMS0, precision=HIGHEST, preferred_element_type=F32)


def kernel(g_hbm, t_hbm, gram_ref, stat_ref, proj_hbm, *scratch):
    it = iter(scratch)
    g, t, raw, gsum = (next(it) for _ in range(4))
    mean, mean_in = {}, {}
    for grp in (PLANE, ALONG):
        mean[grp], mean_in[grp] = next(it), next(it)
    wide, wide_in = next(it), next(it)
    bufs = []
    for part in PARTS:
        b = {"s_out": next(it), "s_in": next(it), "out": next(it), "corr": next(it)}
        b["in"] = [next(it) for _ in part]
        b["acc"] = [None] + [next(it) for _ in part[1:]]
        b["low"] = [None] + [next(it) for _ in part[1:]]
        b["n"] = next(it)
        bufs.append(b)
    p, pb, pb_in, half, hb, hb_in, full = (next(it) for _ in range(7))
    tile, tile_in, every = next(it), next(it), next(it)
    gt, gc_in, gz_in, gh, gh_in, gall = (next(it) for _ in range(6))
    load_sem, send_sem, recv_sem = next(it), next(it), next(it)

    samp, snp = lax.axis_index("samp"), lax.axis_index("snp")
    me = {"x": lax.rem(samp // 2, 4), "y": lax.rem(samp, 2), "z": samp // 8, "h": snp // 2}
    core = lax.rem(snp, 2)

    def index(group, c=me):
        i = 0
        for d in group:
            i = i * SIZE[d] + c[d]
        return i

    def peers(group):
        for ks in itertools.product(*(range(SIZE[d]) for d in group)):
            if any(ks):
                c = dict(me)
                for d, k in zip(group, ks):
                    c[d] = lax.rem(me[d] + k, SIZE[d])
                yield index(group, c), ((c["z"] * 4 + c["x"]) * 2 + c["y"], c["h"] * 2 + core)

    plane, along = list(peers(PLANE)), list(peers(ALONG))
    layer = list(peers(("x", "y", "h")))
    (_, other_half), = peers(("h",))
    other_core = (samp, me["h"] * 2 + (1 - core))
    met = [dev for _, dev in layer + along] + [other_core]

    barrier = pltpu.get_barrier_semaphore()
    for dev in met:
        pl.semaphore_signal(barrier, inc=1, device_id=dev, device_id_type=MESH)
    t_copy = pltpu.make_async_copy(t_hbm, t, load_sem.at[0])
    t_copy.start()
    g_copies = []
    for i in range(len(PARTS)):
        cols = pl.ds(i * PART, PART)
        cp = pltpu.make_async_copy(g_hbm.at[:, cols], g.at[:, cols], load_sem.at[1 + i])
        cp.start()
        g_copies.append(cp)

    count = [0]
    started = []

    def send(src, dst, dev):
        i = count[0]
        count[0] += 1
        cp = pltpu.make_async_remote_copy(
            src_ref=src, dst_ref=dst, send_sem=send_sem.at[i], recv_sem=recv_sem.at[i],
            device_id=dev, device_id_type=MESH)
        cp.start()
        started.append(cp)
        return cp

    def wait(copies):
        for cp in copies:
            cp.wait_recv()

    t_copy.wait()

    def add_rows(i, acc):
        b = t[pl.ds(pl.multiple_of(i * 64, 64), 64), :].astype(F32)
        return acc + jnp.sum(b.reshape(8, 8, TRAITS), axis=0)

    acc = lax.fori_loop(0, ROWS // 64, add_rows, jnp.zeros((8, TRAITS), F32))
    own_mean = jnp.broadcast_to(jnp.sum(acc, axis=0, keepdims=True) * (1.0 / ROWS), (8, TRAITS))
    for grp in (PLANE, ALONG):
        mean[grp][...] = own_mean
    pl.semaphore_wait(barrier, len(met))
    c_plane = [send(mean[PLANE], mean_in[PLANE].at[k], dev) for k, (_, dev) in enumerate(plane)]
    c_along = [] if all(part[0] != ALONG for part in PARTS) else [send(mean[ALONG], mean_in[ALONG].at[k], dev) for k, (_, dev) in enumerate(along)]

    ones_col = jnp.ones((ROWS, 128), BF16)
    ones_row = jnp.ones((8, ROWS), BF16)
    sent = [dict() for _ in PARTS]
    norms = []

    def devices(part, s):
        return {PLANE: plane, ALONG: along}[part[s]] if part[s] in (PLANE, ALONG) else list(peers(part[s]))

    def blocks(part):
        out, n = [], PART
        for grp in part:
            n //= size_of(grp)
            out.append(n)
        return out

    def centred(r, n):
        c = jnp.concatenate([mean[PLANE][...]] * (n // 8), axis=0)
        s = gsum[pl.ds(r, n), :]
        return raw[pl.ds(r, n), :] - jnp.concatenate([s, s], axis=1) * c

    def first_send(i):
        part, b = PARTS[i], bufs[i]
        blk = blocks(part)[0]
        g_copies[i].wait()
        for j in range(PART // 512):
            cols = pl.ds(i * PART + j * 512, 512)
            piece = g[:, cols]
            raw[cols, :] = lax.dot_general(piece, t[...], DIMS0, preferred_element_type=F32)
            gsum[cols, :] = lax.dot_general(piece, ones_col, DIMS0, preferred_element_type=F32)
            sums = jnp.dot(ones_row, piece, preferred_element_type=F32)[:1]
            for q in range(4):
                lane = j * 512 + q * 128
                b["s_out"][lane // blk, pl.ds((lane % blk) // 128, 1), :] = sums[:, q * 128:q * 128 + 128]
        s_cp = []
        for k, (to, dev) in enumerate(devices(part, 0)):
            s_cp.append(send(b["s_out"].at[to], b["s_in"].at[k], dev))
        cps = []
        for k, (to, dev) in enumerate(devices(part, 0)):
            def fill(j, _):
                r = pl.multiple_of(j * 64, 64)
                b["out"][k, pl.ds(r, 64), :] = centred(pl.multiple_of(i * PART + to * blk + r, 64), 64).astype(BF16)
                return 0
            lax.fori_loop(0, blk // 64, fill, 0)
            cps.append(send(b["out"].at[k], b["in"][0].at[k], dev))
        sent[i]["s"], sent[i]["rs"] = s_cp, cps

    def reduce(i, s):
        part, b = PARTS[i], bufs[i]
        blk = blocks(part)[s]
        n = size_of(part[s])
        last = s == len(part) - 1
        mine = index(part[s])
        if s == 0:
            wait(sent[i]["s"])
            grp = part[0]
            if grp == ALONG:
                wait(c_along)
                c_along.clear()
            means, slots = (ALONG, range(7)) if grp == ALONG else (PLANE, SLOTS[grp])
            width = blk // 128
            lines = [b["s_out"].at[mine]] + [b["s_in"].at[k] for k in range(n - 1)]
            sums = jnp.concatenate(
                [jnp.concatenate([ref[pl.ds(q, 1), :] for q in range(width)], axis=1) for ref in lines]
                + [jnp.zeros((8 - n, blk), F32)] * (n < 8), axis=0)
            gaps = jnp.concatenate(
                [mean[means][:1]] + [mean_in[means][k, :1] for k in slots]
                + [jnp.zeros((8 - n, TRAITS), F32)] * (n < 8), axis=0) - wide[1, :1]
            b["corr"][...] = dot_rows(sums, gaps)
        wait(sent[i]["rs"])
        rows = min(blk, 64)

        def body(j, norm):
            r = pl.multiple_of(j * rows, rows)
            if s == 0:
                v = centred(pl.multiple_of(i * PART + mine * blk + r, rows), rows) + b["corr"][pl.ds(r, rows), :]
            else:
                v = b["acc"][s][pl.ds(pl.multiple_of(mine * blk + r, rows), rows), :]
            for k in range(n - 1):
                v = v + b["in"][s][k, pl.ds(r, rows), :].astype(F32)
            if last:
                b["n"][tuple(index(grp) for grp in part)] = v.astype(BF16)
                return norm + jnp.sum(v * v, axis=0, keepdims=True)
            b["acc"][s + 1][pl.ds(r, rows), :] = v
            b["low"][s + 1][pl.ds(r, rows), :] = v.astype(BF16)
            return norm

        norm = lax.fori_loop(0, blk // rows, body, jnp.zeros((1, TRAITS), F32))
        if last:
            norms.append(norm)
            gather(i, s)
            return
        nxt = blocks(part)[s + 1]
        sent[i]["rs"] = [
            send(b["low"][s + 1].at[pl.ds(pl.multiple_of(to * nxt, nxt), nxt), :], b["in"][s + 1].at[k], dev)
            for k, (to, dev) in enumerate(devices(part, s + 1))]

    def gather(i, s):
        part, b = PARTS[i], bufs[i]
        piece = b["n"].at[tuple(index(grp) for grp in part[:s + 1])]
        sent[i]["ag"] = [send(piece, piece, dev) for _, dev in devices(part, s)]

    def project(i):
        v = jnp.dot(g[:, pl.ds(i * PART, PART)], bufs[i]["n"][...].reshape(PART, TRAITS), preferred_element_type=F32)
        if not projected:
            p[...] = v
        else:
            p[...] += v
        projected.append(i)

    projected = []
    for turn, (i, step) in enumerate(order_of()):
        stages = len(PARTS[i])
        if step == 0:
            first_send(i)
        elif step <= stages:
            if turn and wide_send:
                wait(wide_send)
                v = wide[0]
                for k in range(7):
                    v = v + wide_in[k]
                wide[1] = v * (1.0 / GROUPS)
                wide_send.clear()
            reduce(i, step - 1)
        else:
            wait(sent[i]["ag"])
            s = 2 * stages - step - 1
            if s >= 0:
                gather(i, s)
            else:
                project(i)
        if turn == 0:
            wait(c_plane)
            v = mean[PLANE][...]
            for k in range(7):
                v = v + mean_in[PLANE][k]
            wide[0] = v
            wide_send = [send(wide.at[0], wide_in.at[k], dev) for k, (_, dev) in enumerate(along)]

    norm = norms[0]
    for v in norms[1:]:
        norm = norm + v
    own = jnp.sum(p[...], axis=0, keepdims=True) * (1.0 / ROWS)
    tile[0] = jnp.concatenate([own[:, :128], own[:, 128:], norm[:, :128], norm[:, 128:], jnp.zeros((4, 128), F32)], axis=0)
    pb[...] = p[pl.ds(pl.multiple_of((1 - core) * 256, 256), 256), :] - own
    c1 = [send(pb, pb_in, other_core), send(tile.at[0], tile_in.at[0], other_core)]
    wait(c1)
    tile[1] = tile[0] + tile_in[0]
    half[...] = p[pl.ds(pl.multiple_of(core * 256, 256), 256), :] - own + pb_in[...]
    hb[...] = half[pl.ds(pl.multiple_of((1 - me["h"]) * 128, 128), 128), :]
    c2 = [send(hb, hb_in, other_half), send(tile.at[1], tile_in.at[1], other_half)]
    wait(c2)
    tile[2] = tile[1] + tile_in[1]
    mine = half[pl.ds(pl.multiple_of(me["h"] * 128, 128), 128), :] + hb_in[...]
    full[core, me["h"]] = mine

    a_gram = lax.dot_general(mine, mine, DIMS0, precision=HIGHEST, preferred_element_type=F32)
    gt[...] = a_gram.reshape(2, 8, 16, TRAITS)
    g1 = [send(gt.at[1 - core], gc_in, other_core)]
    c3 = [send(full.at[core, me["h"]], full.at[core, me["h"]], other_half)]
    spot = index(PLANE)
    every[spot, me["z"]] = tile[2]
    m1 = [send(every.at[spot, me["z"]], every.at[spot, me["z"]], dev) for _, dev in along]
    wait(g1)
    gc_in[...] = gc_in[...] + gt[core]
    g2 = [send(gc_in.at[to], gz_in.at[k], dev) for k, (to, dev) in enumerate(along)]
    wait(g2)
    v = gc_in[me["z"]]
    for k in range(7):
        v = v + gz_in[k]
    gh[...] = v
    g3 = [send(gh, gh_in.at[k], dev) for k, (_, dev) in enumerate(layer)]
    wait(m1)
    m2 = [send(every.at[spot], every.at[spot], dev) for _, dev in plane]
    wait(c3)
    c4 = [send(full.at[core], full.at[core], other_core)]
    wait(g3)
    v = gh[...]
    for k in range(15):
        v = v + gh_in[k]
    gall[core, me["z"]] = v
    piece = gall.at[core, me["z"]]
    g4 = [send(piece, piece, dev) for _, dev in along]
    wait(c4)
    proj_copy = pltpu.make_async_copy(full, proj_hbm, load_sem.at[0])
    proj_copy.start()
    wait(g4)
    g5 = [send(gall.at[core], gall.at[core], other_core)]
    wait(m2)
    means = jnp.concatenate([every[:, :, r, :].reshape(GROUPS, 128) for r in range(2)], axis=1)
    norm = jnp.concatenate(
        [jnp.sum(every[:, :, r, :].reshape(GROUPS, 128), axis=0, keepdims=True) for r in (2, 3)], axis=1)
    centre = jnp.sum(means, axis=0, keepdims=True) * (1.0 / GROUPS)
    gap = means - centre
    between = dot_rows(gap, gap) * float(ROWS)
    off = jnp.concatenate([tile[2, 0:1], tile[2, 1:2]], axis=1) - centre
    stat_ref[...] = jnp.concatenate([norm, off, jnp.zeros((6, TRAITS), F32)], axis=0)
    wait(g5)
    gram_ref[...] = gall[...].reshape(TRAITS, TRAITS) + between
    for cp in started:
        cp.wait_send()
    proj_copy.wait()
    assert count[0] == COPIES, count[0]


COPIES = 65 + 7 * any(part[0] == ALONG for part in PARTS) + sum(
    size_of(part[0]) - 1 + 2 * sum(size_of(grp) - 1 for grp in part) for part in PARTS)


def scratch_of():
    vmem = pltpu.VMEM
    shapes = [vmem((ROWS, SNPS), BF16), vmem((ROWS, TRAITS), BF16), vmem((SNPS, TRAITS), F32), vmem((SNPS, 128), F32)]
    for _ in range(2):
        shapes += [vmem((8, TRAITS), F32), vmem((7, 8, TRAITS), F32)]
    shapes += [vmem((2, 8, TRAITS), F32), vmem((7, 8, TRAITS), F32)]
    for part in PARTS:
        sizes = [size_of(grp) for grp in part]
        blk, n = [], PART
        for s in sizes:
            n //= s
            blk.append(n)
        shapes += [
            vmem((sizes[0], 8, 128), F32), vmem((sizes[0] - 1, 8, 128), F32),
            vmem((sizes[0] - 1, blk[0], TRAITS), BF16), vmem((blk[0], TRAITS), F32),
        ]
        shapes += [vmem((s - 1, b, TRAITS), BF16) for s, b in zip(sizes, blk)]
        shapes += [vmem((b, TRAITS), F32) for b in blk[:-1]]
        shapes += [vmem((b, TRAITS), BF16) for b in blk[:-1]]
        shapes += [vmem((*sizes, OWN, TRAITS), BF16)]
    shapes += [
        vmem((ROWS, TRAITS), F32), vmem((256, TRAITS), F32), vmem((256, TRAITS), F32), vmem((256, TRAITS), F32),
        vmem((128, TRAITS), F32), vmem((128, TRAITS), F32), vmem((2, 2, 128, TRAITS), F32),
        vmem((3, 8, 128), F32), vmem((2, 8, 128), F32), vmem((8, 8, 8, 128), F32),
        vmem((2, 8, 16, TRAITS), F32), vmem((8, 16, TRAITS), F32), vmem((7, 16, TRAITS), F32), vmem((16, TRAITS), F32),
        vmem((15, 16, TRAITS), F32), vmem((2, 8, 16, TRAITS), F32),
        pltpu.SemaphoreType.DMA((5,)), pltpu.SemaphoreType.DMA((COPIES,)), pltpu.SemaphoreType.DMA((COPIES,)),
    ]
    return shapes


def finish(gram_ref, stat_ref, proj_ref, basis_ref, fit_ref, cov_ref, score_ref):
    gram = gram_ref[...]
    norm_row, off = stat_ref[0:1, :], stat_ref[1:2, :]
    square = (TRAITS, TRAITS)
    eye = lax.broadcasted_iota(jnp.int32, square, 0) == lax.broadcasted_iota(jnp.int32, square, 1)
    diag_row = jnp.sum(jnp.where(eye, gram, 0.0), axis=0, keepdims=True)
    step_row = norm_row / (diag_row + (SAMPLES / 8.0) * norm_row)
    step_col = jnp.sum(jnp.where(eye, jnp.broadcast_to(step_row, square), 0.0), axis=1, keepdims=True)
    cov = step_col * gram * step_row * (1.0 / SAMPLES)
    cov_ref[...] = cov
    spread = jnp.sum(step_row * step_row * diag_row, axis=1, keepdims=True) * (1.0 / SAMPLES) + 1e-6
    dims1 = (((1,), (1,)), ((), ()))
    loading = lax.dot_general(basis_ref[...], cov, (((1,), (1,)), ((), ())), precision=HIGHEST,
                              preferred_element_type=F32) * (TRAITS / spread)
    high = loading.astype(BF16)
    low = (loading - high.astype(F32)).astype(BF16)
    f = ((proj_ref[...].reshape(ROWS, TRAITS) + off) * step_row).astype(BF16)
    fit_ref[...] = f
    score_ref[...] = (lax.dot_general(high, f, dims1, preferred_element_type=F32)
                      + lax.dot_general(low, f, dims1, preferred_element_type=F32))


def local(genotypes, traits, trait_basis):
    anywhere = pl.BlockSpec(memory_space=pl.ANY)
    inside = pl.BlockSpec(memory_space=pltpu.VMEM)
    gram, stat, proj = pl.pallas_call(
        kernel,
        out_shape=(
            jax.ShapeDtypeStruct((TRAITS, TRAITS), F32),
            jax.ShapeDtypeStruct((8, TRAITS), F32),
            jax.ShapeDtypeStruct((2, 2, 128, TRAITS), F32),
        ),
        in_specs=[anywhere, anywhere],
        out_specs=(inside, inside, anywhere),
        scratch_shapes=scratch_of(),
        compiler_params=pltpu.CompilerParams(
            collective_id=0, has_side_effects=True, vmem_limit_bytes=56 * 2**20),
    )(genotypes, traits)
    fitted, covariance, scores = pl.pallas_call(
        finish,
        out_shape=(
            jax.ShapeDtypeStruct((ROWS, TRAITS), BF16),
            jax.ShapeDtypeStruct((TRAITS, TRAITS), F32),
            jax.ShapeDtypeStruct((RANK, ROWS), F32),
        ),
        in_specs=[inside] * 4,
        out_specs=(inside, inside, inside),
    )(gram, stat, proj, trait_basis.T)
    return fitted, covariance, scores.T


def solution(mesh):
    return jax.shard_map(
        local,
        mesh=mesh,
        in_specs=(P("samp", "snp"), P("samp", None), P()),
        out_specs=(P("samp", None), P(), P("samp", None)),
        check_vma=False,
    )
```

```python
import itertools

import jax
import jax.numpy as jnp
from jax import lax
from jax.experimental import pallas as pl
from jax.experimental.pallas import tpu as pltpu
from jax.sharding import PartitionSpec as P

MESH = pl.DeviceIdType.MESH
F32, BF16 = jnp.float32, jnp.bfloat16
HIGHEST = lax.Precision.HIGHEST
SIZE = {"x": 4, "y": 2, "z": 8, "h": 2}
ROWS, SNPS, TRAITS, RANK = 512, 4096, 256, 64
GROUPS = 64
SAMPLES = GROUPS * ROWS
DIMS0 = (((0,), (0,)), ((), ()))
PLANE, ALONG = ("x", "y"), ("z",)
BLOCKS = ((("y",), ("x",), ALONG), (("x",), ("y",), ALONG), (ALONG, PLANE), (("y",), ("x",), ALONG))
PART = SNPS // len(BLOCKS)
OWN = PART // GROUPS
WIDTH = 128
PARTS = tuple((groups, b, h) for b, groups in enumerate(BLOCKS) for h in range(2))
ORDER = (
    (3, 0), (1, 0), (2, 0), (4, 0), (0, 0), (7, 0), (5, 0), (1, 1), (6, 0), (0, 1), (2, 1), (7, 1),
    (3, 1), (0, 2), (4, 1), (1, 2), (6, 1), (2, 2), (3, 2), (7, 2), (0, 3), (4, 2), (5, 1), (6, 2),
    (1, 3), (2, 3), (3, 3), (0, 4), (6, 3), (1, 4), (7, 3), (5, 2), (2, 4), (3, 4), (4, 3), (0, 5),
    (6, 4), (1, 5), (7, 4), (5, 3), (3, 5), (2, 5), (6, 5), (4, 4), (7, 5), (6, 6), (3, 6), (2, 6),
    (1, 6), (0, 6), (5, 4), (7, 6),
)
SLOTS = {PLANE: (0, 1, 2, 3, 4, 5, 6), ("x",): (1, 3, 5), ("y",): (0,)}


def size_of(group):
    n = 1
    for d in group:
        n *= SIZE[d]
    return n


def dot_rows(a, b):
    return lax.dot_general(a, b, DIMS0, precision=HIGHEST, preferred_element_type=F32)


def kernel(g_hbm, t_hbm, gram_ref, stat_ref, proj_hbm, *scratch):
    it = iter(scratch)
    g, t, raw, gsum = (next(it) for _ in range(4))
    mean, mean_in = {}, {}
    for grp in (PLANE, ALONG):
        mean[grp], mean_in[grp] = next(it), next(it)
    wide, wide_in = next(it), next(it)
    tables = [(next(it), next(it), next(it)) for _ in BLOCKS]
    bufs = []
    for part, _, _ in PARTS:
        b = {"out": next(it), "corr": next(it)}
        b["in"] = [next(it) for _ in part]
        b["acc"] = [None] + [next(it) for _ in part[1:]]
        b["low"] = [None] + [next(it) for _ in part[1:]]
        bufs.append(b)
    p, pb, pb_in, hb, hb_in, full = (next(it) for _ in range(6))
    tile, tile_in, every = next(it), next(it), next(it)
    gt, gc_in, gh_in, gz, gz_in, gall = (next(it) for _ in range(6))
    load_sem, send_sem, recv_sem = next(it), next(it), next(it)

    samp, snp = lax.axis_index("samp"), lax.axis_index("snp")
    me = {"x": lax.rem(samp // 2, 4), "y": lax.rem(samp, 2), "z": samp // 8, "h": snp // 2}
    core = lax.rem(snp, 2)

    def index(group, c=me):
        i = 0
        for d in group:
            i = i * SIZE[d] + c[d]
        return i

    def peers(group):
        for ks in itertools.product(*(range(SIZE[d]) for d in group)):
            if any(ks):
                c = dict(me)
                for d, k in zip(group, ks):
                    c[d] = lax.rem(me[d] + k, SIZE[d])
                yield index(group, c), ((c["z"] * 4 + c["x"]) * 2 + c["y"], c["h"] * 2 + core)

    plane, along = list(peers(PLANE)), list(peers(ALONG))
    layer = list(peers(("x", "y", "h")))
    (_, other_half), = peers(("h",))
    other_core = (samp, me["h"] * 2 + (1 - core))
    met = [dev for _, dev in layer + along] + [other_core]

    barrier = pltpu.get_barrier_semaphore()
    for dev in met:
        pl.semaphore_signal(barrier, inc=1, device_id=dev, device_id_type=MESH)
    t_copy = pltpu.make_async_copy(t_hbm, t, load_sem.at[0])
    t_copy.start()
    g_copies = []
    for i in range(len(BLOCKS)):
        cols = pl.ds(i * PART, PART)
        cp = pltpu.make_async_copy(g_hbm.at[:, cols], g.at[:, cols], load_sem.at[1 + i])
        cp.start()
        g_copies.append(cp)

    count = [0]
    started = []

    def send(src, dst, dev):
        i = count[0]
        count[0] += 1
        cp = pltpu.make_async_remote_copy(
            src_ref=src, dst_ref=dst, send_sem=send_sem.at[i], recv_sem=recv_sem.at[i],
            device_id=dev, device_id_type=MESH)
        cp.start()
        started.append(cp)
        return cp

    def wait(copies):
        for cp in copies:
            cp.wait_recv()

    t_copy.wait()

    def add_rows(i, acc):
        b = t[pl.ds(pl.multiple_of(i * 64, 64), 64), :].astype(F32)
        return acc + jnp.sum(b.reshape(8, 8, TRAITS), axis=0)

    acc = lax.fori_loop(0, ROWS // 64, add_rows, jnp.zeros((8, TRAITS), F32))
    own_mean = jnp.sum(acc, axis=0, keepdims=True) * (1.0 / ROWS)
    for grp in (PLANE, ALONG):
        mean[grp][...] = own_mean
    pl.semaphore_wait(barrier, len(met))
    c_plane = [send(mean[PLANE], mean_in[PLANE].at[k], dev) for k, (_, dev) in enumerate(plane)]
    c_along = [] if all(part[0] != ALONG for part in BLOCKS) else [send(mean[ALONG], mean_in[ALONG].at[k], dev) for k, (_, dev) in enumerate(along)]

    ones_col = jnp.ones((ROWS, 128), BF16)
    ones_row = jnp.ones((8, ROWS), BF16)
    sent = [dict() for _ in PARTS]
    norms = [[], []]
    made, s_sent = set(), {}

    def devices(part, s):
        return {PLANE: plane, ALONG: along}[part[s]] if part[s] in (PLANE, ALONG) else list(peers(part[s]))

    def blocks(part):
        out, n = [], PART
        for grp in part:
            n //= size_of(grp)
            out.append(n)
        return out

    def centred(r, n, h):
        cols = pl.ds(h * WIDTH, WIDTH)
        return raw[pl.ds(r, n), cols] - gsum[pl.ds(r, n), :] * mean[PLANE][:, cols]

    def make(block):
        part = BLOCKS[block]
        blk = blocks(part)[0]
        s_out, s_in, _ = tables[block]
        g_copies[block].wait()
        for j in range(PART // 512):
            cols = pl.ds(block * PART + j * 512, 512)
            piece = g[:, cols]
            raw[cols, :] = lax.dot_general(piece, t[...], DIMS0, preferred_element_type=F32)
            gsum[cols, :] = lax.dot_general(piece, ones_col, DIMS0, preferred_element_type=F32)
            sums = jnp.dot(ones_row, piece, preferred_element_type=F32)[:1]
            for q in range(4):
                lane = j * 512 + q * 128
                s_out[lane // blk, pl.ds((lane % blk) // 128, 1), :] = sums[:, q * 128:q * 128 + 128]
        s_sent[block] = [send(s_out.at[to], s_in.at[k], dev) for k, (to, dev) in enumerate(devices(part, 0))]

    def first_send(i):
        (part, block, h), b = PARTS[i], bufs[i]
        blk = blocks(part)[0]
        if block not in made:
            made.add(block)
            make(block)
        cps = []
        for k, (to, dev) in enumerate(devices(part, 0)):
            def fill(j, _):
                r = pl.multiple_of(j * 128, 128)
                v = centred(pl.multiple_of(block * PART + to * blk + r, 128), 128, h)
                b["out"][k, pl.ds(r, 128), :] = v.astype(BF16)
                return 0
            lax.fori_loop(0, blk // 128, fill, 0)
            cps.append(send(b["out"].at[k], b["in"][0].at[k], dev))
        sent[i]["rs"] = cps

    def reduce(i, s):
        (part, block, h), b = PARTS[i], bufs[i]
        blk = blocks(part)[s]
        n = size_of(part[s])
        last = s == len(part) - 1
        mine = index(part[s])
        cols = pl.ds(h * WIDTH, WIDTH)
        if s == 0:
            wait(s_sent.pop(block, []))
            grp = part[0]
            if grp == ALONG:
                wait(c_along)
                c_along.clear()
            means, slots = (ALONG, range(7)) if grp == ALONG else (PLANE, SLOTS[grp])
            s_out, s_in, _ = tables[block]
            lines = [s_out.at[mine]] + [s_in.at[k] for k in range(n - 1)]
            sums = jnp.concatenate(
                [jnp.concatenate([ref[pl.ds(q, 1), :] for q in range(blk // 128)], axis=1) for ref in lines]
                + [jnp.zeros((8 - n, blk), F32)] * (n < 8), axis=0)
            gaps = jnp.concatenate(
                [mean[means][:1, cols]] + [mean_in[means][k, :1, cols] for k in slots]
                + [jnp.zeros((8 - n, WIDTH), F32)] * (n < 8), axis=0) - wide[1, :1, cols]
            b["corr"][...] = dot_rows(sums, gaps)
        wait(sent[i]["rs"])
        rows = min(blk, 128)

        def body(j, norm):
            r = pl.multiple_of(j * rows, rows)
            if s == 0:
                v = centred(pl.multiple_of(block * PART + mine * blk + r, rows), rows, h) + b["corr"][pl.ds(r, rows), :]
            else:
                v = b["acc"][s][pl.ds(pl.multiple_of(mine * blk + r, rows), rows), :]
            for k in range(n - 1):
                v = v + b["in"][s][k, pl.ds(r, rows), :].astype(F32)
            if last:
                tables[block][2][(*(index(grp) for grp in part), slice(None), cols)] = v.astype(BF16)
                return norm + jnp.sum(v * v, axis=0, keepdims=True)
            b["acc"][s + 1][pl.ds(r, rows), :] = v
            b["low"][s + 1][pl.ds(r, rows), :] = v.astype(BF16)
            return norm

        norm = jnp.zeros((1, WIDTH), F32)
        if blk == rows:
            norm = body(0, norm)
        else:
            norm = lax.fori_loop(0, blk // rows, body, norm)
        if last:
            norms[h].append(norm)
            gather(i, s)
            return
        nxt = blocks(part)[s + 1]
        sent[i]["rs"] = [
            send(b["low"][s + 1].at[pl.ds(pl.multiple_of(to * nxt, nxt), nxt), :], b["in"][s + 1].at[k], dev)
            for k, (to, dev) in enumerate(devices(part, s + 1))]

    def gather(i, s):
        part, block, h = PARTS[i]
        at = tuple(index(grp) for grp in part[:s + 1]) + (slice(None),) * (len(part) - s)
        piece = tables[block][2].at[(*at, pl.ds(h * WIDTH, WIDTH))]
        sent[i]["ag"] = [send(piece, piece, dev) for _, dev in devices(part, s)]

    def project(i):
        block = PARTS[i][1]
        if block not in ready:
            ready.add(block)
            return
        n = tables[block][2][...].reshape(PART, TRAITS)
        v = jnp.dot(g[:, pl.ds(block * PART, PART)], n, preferred_element_type=F32)
        if not projected:
            p[...] = v
        else:
            p[...] += v
        projected.append(block)

    ready = set()
    projected = []
    for turn, (i, step) in enumerate(ORDER):
        stages = len(PARTS[i][0])
        if step == 0:
            first_send(i)
        elif step <= stages:
            if turn and wide_send:
                wait(wide_send)
                v = wide[0]
                for k in range(7):
                    v = v + wide_in[k]
                wide[1] = v * (1.0 / GROUPS)
                wide_send.clear()
            reduce(i, step - 1)
        else:
            wait(sent[i]["ag"])
            s = 2 * stages - step - 1
            if s >= 0:
                gather(i, s)
            else:
                project(i)
        if turn == 0:
            wait(c_plane)
            v = mean[PLANE][...]
            for k in range(7):
                v = v + mean_in[PLANE][k]
            wide[0] = v
            wide_send = [send(wide.at[0], wide_in.at[k], dev) for k, (_, dev) in enumerate(along)]

    own = jnp.sum(p[...], axis=0, keepdims=True) * (1.0 / ROWS)
    lines = [own[:, :128], own[:, 128:]]
    for h in range(2):
        norm = norms[h][0]
        for v in norms[h][1:]:
            norm = norm + v
        lines.append(norm)
    tile[0] = jnp.concatenate(lines, axis=0)

    def rows_at(c, h):
        return pl.ds(pl.multiple_of(c * 256 + h * 128, 128), 128)

    halves = (1 - me["h"], me["h"])
    c1 = []
    for j, h in enumerate(halves):
        pb[j] = p[rows_at(1 - core, h), :] - own
        c1.append(send(pb.at[j], pb_in.at[j], other_core))
    c1.append(send(tile.at[0], tile_in.at[0], other_core))
    wait(c1[:1])
    hb[...] = (p[rows_at(core, halves[0]), :] - own + pb_in[0]).astype(BF16)
    c2 = [send(hb, hb_in, other_half)]
    wait(c1[1:])
    tile[1] = tile[0] + tile_in[0]
    c2.append(send(tile.at[1], tile_in.at[1], other_half))
    near = p[rows_at(core, halves[1]), :] - own + pb_in[1]
    wait(c2[:1])
    mine = near + hb_in[...].astype(F32)
    full[core, me["h"]] = mine
    c3 = [send(full.at[core, me["h"]], full.at[core, me["h"]], other_half)]

    for c in (1 - core, core):
        cols = full[core, me["h"], :, pl.ds(pl.multiple_of(c * 128, 128), 128)]
        gt[c] = dot_rows(cols, mine).reshape(16, 8, TRAITS)
        if c is not core:
            g1 = [send(gt.at[c], gc_in, other_core)]
    wait(c2[1:])
    tile[2] = tile[1] + tile_in[1]
    spot = index(PLANE)
    every[me["z"], spot] = tile[2]
    m1 = [send(every.at[me["z"], spot], every.at[me["z"], spot], dev) for _, dev in plane]
    wait(g1)
    gc_in[...] = gc_in[...] + gt[core]
    g2 = [send(gc_in.at[to], gh_in.at[k], dev) for k, (to, dev) in enumerate(layer)]
    wait(m1)
    m2 = [send(every.at[me["z"]], every.at[me["z"]], dev) for _, dev in along]
    wait(g2)
    mid = index(("x", "y", "h"))
    v = gc_in[mid]
    for k in range(15):
        v = v + gh_in[k]
    gz[...] = v
    g3 = [send(gz, gz_in.at[k], dev) for k, (_, dev) in enumerate(along)]
    wait(g3)
    v = gz[...]
    for k in range(7):
        v = v + gz_in[k]
    gall[core, mid] = v
    piece = gall.at[core, mid]
    g4 = [send(piece, piece, dev) for _, dev in layer]
    wait(c3)
    c4 = [send(full.at[core], full.at[core], other_core)]
    wait(c4)
    proj_copy = pltpu.make_async_copy(full, proj_hbm, load_sem.at[0])
    proj_copy.start()
    wait(g4)
    g5 = [send(gall.at[core], gall.at[core], other_core)]
    wait(m2)
    means = jnp.concatenate([every[:, :, r, :].reshape(GROUPS, 128) for r in range(2)], axis=1)
    norm = jnp.concatenate(
        [jnp.sum(every[:, :, r, :].reshape(GROUPS, 128), axis=0, keepdims=True) for r in (2, 3)], axis=1)
    centre = jnp.sum(means, axis=0, keepdims=True) * (1.0 / GROUPS)
    gap = means - centre
    between = dot_rows(gap, gap) * float(ROWS)
    off = jnp.concatenate([tile[2, 0:1], tile[2, 1:2]], axis=1) - centre
    stat_ref[...] = jnp.concatenate([norm, off, jnp.zeros((6, TRAITS), F32)], axis=0)
    wait(g5)
    gram_ref[...] = gall[...].reshape(TRAITS, TRAITS) + between
    for cp in started:
        cp.wait_send()
    proj_copy.wait()
    assert count[0] == COPIES, count[0]


COPIES = 74 + 7 * any(part[0] == ALONG for part in BLOCKS) + sum(
    size_of(part[0]) - 1 + 4 * sum(size_of(grp) - 1 for grp in part) for part in BLOCKS)


def scratch_of():
    vmem = pltpu.VMEM
    shapes = [vmem((ROWS, SNPS), BF16), vmem((ROWS, TRAITS), BF16), vmem((SNPS, TRAITS), F32), vmem((SNPS, 128), F32)]
    for _ in range(2):
        shapes += [vmem((1, TRAITS), F32), vmem((7, 1, TRAITS), F32)]
    shapes += [vmem((2, 1, TRAITS), F32), vmem((7, 1, TRAITS), F32)]
    for part in BLOCKS:
        sizes = [size_of(grp) for grp in part]
        shapes += [vmem((sizes[0], 8, 128), F32), vmem((sizes[0] - 1, 8, 128), F32), vmem((*sizes, OWN, TRAITS), BF16)]
    for part, _, _ in PARTS:
        sizes = [size_of(grp) for grp in part]
        blk, n = [], PART
        for s in sizes:
            n //= s
            blk.append(n)
        shapes += [vmem((sizes[0] - 1, blk[0], WIDTH), BF16), vmem((blk[0], WIDTH), F32)]
        shapes += [vmem((s - 1, b, WIDTH), BF16) for s, b in zip(sizes, blk)]
        shapes += [vmem((b, WIDTH), F32) for b in blk[:-1]]
        shapes += [vmem((b, WIDTH), BF16) for b in blk[:-1]]
    shapes += [
        vmem((ROWS, TRAITS), F32), vmem((2, 128, TRAITS), F32), vmem((2, 128, TRAITS), F32),
        vmem((128, TRAITS), BF16), vmem((128, TRAITS), BF16), vmem((2, 2, 128, TRAITS), F32),
        vmem((3, 4, 128), F32), vmem((2, 4, 128), F32), vmem((8, 8, 4, 128), F32),
        vmem((2, 16, 8, TRAITS), F32), vmem((16, 8, TRAITS), F32), vmem((15, 8, TRAITS), F32), vmem((8, TRAITS), F32),
        vmem((7, 8, TRAITS), F32), vmem((2, 16, 8, TRAITS), F32),
        pltpu.SemaphoreType.DMA((5,)), pltpu.SemaphoreType.DMA((COPIES,)), pltpu.SemaphoreType.DMA((COPIES,)),
    ]
    return shapes


def finish(gram_ref, stat_ref, proj_ref, basis_ref, fit_ref, cov_ref, score_ref):
    gram = gram_ref[...]
    norm_row, off = stat_ref[0:1, :], stat_ref[1:2, :]
    square = (TRAITS, TRAITS)
    eye = lax.broadcasted_iota(jnp.int32, square, 0) == lax.broadcasted_iota(jnp.int32, square, 1)
    diag_row = jnp.sum(jnp.where(eye, gram, 0.0), axis=0, keepdims=True)
    step_row = norm_row / (diag_row + (SAMPLES / 8.0) * norm_row)
    step_col = jnp.sum(jnp.where(eye, jnp.broadcast_to(step_row, square), 0.0), axis=1, keepdims=True)
    cov = step_col * gram * step_row * (1.0 / SAMPLES)
    cov_ref[...] = cov
    spread = jnp.sum(step_row * step_row * diag_row, axis=1, keepdims=True) * (1.0 / SAMPLES) + 1e-6
    dims1 = (((1,), (1,)), ((), ()))
    loading = lax.dot_general(basis_ref[...], cov, (((1,), (1,)), ((), ())), precision=HIGHEST,
                              preferred_element_type=F32) * (TRAITS / spread)
    high = loading.astype(BF16)
    low = (loading - high.astype(F32)).astype(BF16)
    f = ((proj_ref[...].reshape(ROWS, TRAITS) + off) * step_row).astype(BF16)
    fit_ref[...] = f
    score_ref[...] = (lax.dot_general(high, f, dims1, preferred_element_type=F32)
                      + lax.dot_general(low, f, dims1, preferred_element_type=F32))


def local(genotypes, traits, trait_basis):
    anywhere = pl.BlockSpec(memory_space=pl.ANY)
    inside = pl.BlockSpec(memory_space=pltpu.VMEM)
    gram, stat, proj = pl.pallas_call(
        kernel,
        out_shape=(
            jax.ShapeDtypeStruct((TRAITS, TRAITS), F32),
            jax.ShapeDtypeStruct((8, TRAITS), F32),
            jax.ShapeDtypeStruct((2, 2, 128, TRAITS), F32),
        ),
        in_specs=[anywhere, anywhere],
        out_specs=(inside, inside, anywhere),
        scratch_shapes=scratch_of(),
        compiler_params=pltpu.CompilerParams(
            collective_id=0, has_side_effects=True, vmem_limit_bytes=56 * 2**20),
    )(genotypes, traits)
    fitted, covariance, scores = pl.pallas_call(
        finish,
        out_shape=(
            jax.ShapeDtypeStruct((ROWS, TRAITS), BF16),
            jax.ShapeDtypeStruct((TRAITS, TRAITS), F32),
            jax.ShapeDtypeStruct((RANK, ROWS), F32),
        ),
        in_specs=[inside] * 4,
        out_specs=(inside, inside, inside),
    )(gram, stat, proj, trait_basis.T)
    return fitted, covariance, scores.T


def solution(mesh):
    return jax.shard_map(
        local,
        mesh=mesh,
        in_specs=(P("samp", "snp"), P("samp", None), P()),
        out_specs=(P("samp", None), P(), P("samp", None)),
        check_vma=False,
    )
```

```python
import itertools

import jax
import jax.numpy as jnp
from jax import lax
from jax.experimental import pallas as pl
from jax.experimental.pallas import tpu as pltpu
from jax.sharding import PartitionSpec as P

MESH = pl.DeviceIdType.MESH
F32, BF16 = jnp.float32, jnp.bfloat16
HIGHEST = lax.Precision.HIGHEST
SIZE = {"x": 4, "y": 2, "z": 8, "h": 2}
ROWS, SNPS, TRAITS, RANK = 512, 4096, 256, 64
GROUPS = 64
SAMPLES = GROUPS * ROWS
DIMS0 = (((0,), (0,)), ((), ()))
PLANE, ALONG = ("x", "y"), ("z",)
BLOCKS = ((("y",), ("x",), ALONG), (("x",), ("y",), ALONG), (ALONG, PLANE), (("y",), ("x",), ALONG))
PART = SNPS // len(BLOCKS)
OWN = PART // GROUPS
WIDTH = 128
PARTS = tuple((groups, b, h) for b, groups in enumerate(BLOCKS) for h in range(2))
ORDER = (
    (3, 0), (1, 0), (2, 0), (4, 0), (0, 0), (7, 0), (5, 0), (1, 1), (6, 0), (0, 1), (2, 1), (7, 1),
    (3, 1), (0, 2), (4, 1), (1, 2), (6, 1), (2, 2), (3, 2), (7, 2), (0, 3), (4, 2), (5, 1), (6, 2),
    (1, 3), (2, 3), (3, 3), (0, 4), (6, 3), (1, 4), (7, 3), (5, 2), (2, 4), (3, 4), (4, 3), (0, 5),
    (6, 4), (1, 5), (7, 4), (5, 3), (3, 5), (2, 5), (6, 5), (4, 4), (7, 5), (6, 6), (3, 6), (2, 6),
    (1, 6), (0, 6), (5, 4), (7, 6),
)
SLOTS = {PLANE: (0, 1, 2, 3, 4, 5, 6), ("x",): (1, 3, 5), ("y",): (0,)}


def size_of(group):
    n = 1
    for d in group:
        n *= SIZE[d]
    return n


def dot_rows(a, b):
    return lax.dot_general(a, b, DIMS0, precision=HIGHEST, preferred_element_type=F32)


def kernel(g_hbm, t_hbm, gram_ref, stat_ref, proj_hbm, *scratch):
    it = iter(scratch)
    g, t, raw, gsum = (next(it) for _ in range(4))
    mean, mean_in = {}, {}
    for grp in (PLANE, ALONG):
        mean[grp], mean_in[grp] = next(it), next(it)
    wide, wide_in = next(it), next(it)
    tables = [(next(it), next(it), next(it)) for _ in BLOCKS]
    bufs = []
    for part, _, _ in PARTS:
        b = {"out": next(it), "corr": next(it)}
        b["in"] = [next(it) for _ in part]
        b["acc"] = [None] + [next(it) for _ in part[1:]]
        b["low"] = [None] + [next(it) for _ in part[1:]]
        bufs.append(b)
    p, pb, pb_in, hb, hb_in, full = (next(it) for _ in range(6))
    tile, tile_in, every = next(it), next(it), next(it)
    gt, gc_in, gh_in, gz, gz_in, gall = (next(it) for _ in range(6))
    load_sem, send_sem, recv_sem = next(it), next(it), next(it)

    samp, snp = lax.axis_index("samp"), lax.axis_index("snp")
    me = {"x": lax.rem(samp // 2, 4), "y": lax.rem(samp, 2), "z": samp // 8, "h": snp // 2}
    core = lax.rem(snp, 2)

    def index(group, c=me):
        i = 0
        for d in group:
            i = i * SIZE[d] + c[d]
        return i

    def peers(group):
        for ks in itertools.product(*(range(SIZE[d]) for d in group)):
            if any(ks):
                c = dict(me)
                for d, k in zip(group, ks):
                    c[d] = lax.rem(me[d] + k, SIZE[d])
                yield index(group, c), ((c["z"] * 4 + c["x"]) * 2 + c["y"], c["h"] * 2 + core)

    plane, along = list(peers(PLANE)), list(peers(ALONG))
    layer = list(peers(("x", "y", "h")))
    (_, other_half), = peers(("h",))
    other_core = (samp, me["h"] * 2 + (1 - core))
    met = [dev for _, dev in layer + along] + [other_core]

    t_copy = pltpu.make_async_copy(t_hbm, t, load_sem.at[0])
    t_copy.start()
    g_copies = {}
    for i, step in ORDER:
        block = PARTS[i][1]
        if step == 0 and block not in g_copies:
            cols = pl.ds(block * PART, PART)
            g_copies[block] = pltpu.make_async_copy(g_hbm.at[:, cols], g.at[:, cols], load_sem.at[1 + block])
            g_copies[block].start()

    barrier = pltpu.get_barrier_semaphore()
    for dev in met:
        pl.semaphore_signal(barrier, inc=1, device_id=dev, device_id_type=MESH)
    count = [0]
    started = []

    def send(src, dst, dev):
        i = count[0]
        count[0] += 1
        cp = pltpu.make_async_remote_copy(
            src_ref=src, dst_ref=dst, send_sem=send_sem.at[i], recv_sem=recv_sem.at[i],
            device_id=dev, device_id_type=MESH)
        cp.start()
        started.append(cp)
        return cp

    def wait(copies):
        for cp in copies:
            cp.wait_recv()

    t_copy.wait()

    def add_rows(i, acc):
        b = t[pl.ds(pl.multiple_of(i * 64, 64), 64), :].astype(F32)
        return acc + jnp.sum(b.reshape(8, 8, TRAITS), axis=0)

    acc = lax.fori_loop(0, ROWS // 64, add_rows, jnp.zeros((8, TRAITS), F32))
    own_mean = jnp.sum(acc, axis=0, keepdims=True) * (1.0 / ROWS)
    for grp in (PLANE, ALONG):
        mean[grp][...] = own_mean
    pl.semaphore_wait(barrier, len(met))
    c_plane = [send(mean[PLANE], mean_in[PLANE].at[k], dev) for k, (_, dev) in enumerate(plane)]
    c_along = [] if all(part[0] != ALONG for part in BLOCKS) else [send(mean[ALONG], mean_in[ALONG].at[k], dev) for k, (_, dev) in enumerate(along)]

    ones_col = jnp.ones((ROWS, 128), BF16)
    ones_row = jnp.ones((8, ROWS), BF16)
    sent = [dict() for _ in PARTS]
    norms = [[], []]
    made, s_sent = set(), {}

    def devices(part, s):
        return {PLANE: plane, ALONG: along}[part[s]] if part[s] in (PLANE, ALONG) else list(peers(part[s]))

    def blocks(part):
        out, n = [], PART
        for grp in part:
            n //= size_of(grp)
            out.append(n)
        return out

    def centred(r, n, h):
        cols = pl.ds(h * WIDTH, WIDTH)
        return raw[pl.ds(r, n), cols] - gsum[pl.ds(r, n), :] * mean[PLANE][:, cols]

    def make(block):
        part = BLOCKS[block]
        blk = blocks(part)[0]
        s_out, s_in, _ = tables[block]
        g_copies[block].wait()
        for j in range(PART // 512):
            cols = pl.ds(block * PART + j * 512, 512)
            piece = g[:, cols]
            raw[cols, :] = lax.dot_general(piece, t[...], DIMS0, preferred_element_type=F32)
            gsum[cols, :] = lax.dot_general(piece, ones_col, DIMS0, preferred_element_type=F32)
            sums = jnp.dot(ones_row, piece, preferred_element_type=F32)[:1]
            for q in range(4):
                lane = j * 512 + q * 128
                s_out[lane // blk, pl.ds((lane % blk) // 128, 1), :] = sums[:, q * 128:q * 128 + 128]
        s_sent[block] = [send(s_out.at[to], s_in.at[k], dev) for k, (to, dev) in enumerate(devices(part, 0))]

    def first_send(i):
        (part, block, h), b = PARTS[i], bufs[i]
        blk = blocks(part)[0]
        if block not in made:
            made.add(block)
            make(block)
        cps = []
        for k, (to, dev) in enumerate(devices(part, 0)):
            def fill(j, _):
                r = pl.multiple_of(j * 128, 128)
                v = centred(pl.multiple_of(block * PART + to * blk + r, 128), 128, h)
                b["out"][k, pl.ds(r, 128), :] = v.astype(BF16)
                return 0
            lax.fori_loop(0, blk // 128, fill, 0)
            cps.append(send(b["out"].at[k], b["in"][0].at[k], dev))
        sent[i]["rs"] = cps

    def reduce(i, s):
        (part, block, h), b = PARTS[i], bufs[i]
        blk = blocks(part)[s]
        n = size_of(part[s])
        last = s == len(part) - 1
        mine = index(part[s])
        cols = pl.ds(h * WIDTH, WIDTH)
        if s == 0:
            wait(s_sent.pop(block, []))
            grp = part[0]
            if grp == ALONG:
                wait(c_along)
                c_along.clear()
            means, slots = (ALONG, range(7)) if grp == ALONG else (PLANE, SLOTS[grp])
            s_out, s_in, _ = tables[block]
            lines = [s_out.at[mine]] + [s_in.at[k] for k in range(n - 1)]
            sums = jnp.concatenate(
                [jnp.concatenate([ref[pl.ds(q, 1), :] for q in range(blk // 128)], axis=1) for ref in lines]
                + [jnp.zeros((8 - n, blk), F32)] * (n < 8), axis=0)
            gaps = jnp.concatenate(
                [mean[means][:1, cols]] + [mean_in[means][k, :1, cols] for k in slots]
                + [jnp.zeros((8 - n, WIDTH), F32)] * (n < 8), axis=0) - wide[1, :1, cols]
            b["corr"][...] = dot_rows(sums, gaps)
        wait(sent[i]["rs"])
        rows = min(blk, 128)

        def body(j, norm):
            r = pl.multiple_of(j * rows, rows)
            if s == 0:
                v = centred(pl.multiple_of(block * PART + mine * blk + r, rows), rows, h) + b["corr"][pl.ds(r, rows), :]
            else:
                v = b["acc"][s][pl.ds(pl.multiple_of(mine * blk + r, rows), rows), :]
            for k in range(n - 1):
                v = v + b["in"][s][k, pl.ds(r, rows), :].astype(F32)
            if last:
                tables[block][2][(*(index(grp) for grp in part), slice(None), cols)] = v.astype(BF16)
                return norm + jnp.sum(v * v, axis=0, keepdims=True)
            b["acc"][s + 1][pl.ds(r, rows), :] = v
            b["low"][s + 1][pl.ds(r, rows), :] = v.astype(BF16)
            return norm

        norm = jnp.zeros((1, WIDTH), F32)
        if blk == rows:
            norm = body(0, norm)
        else:
            norm = lax.fori_loop(0, blk // rows, body, norm)
        if last:
            norms[h].append(norm)
            gather(i, s)
            return
        nxt = blocks(part)[s + 1]
        sent[i]["rs"] = [
            send(b["low"][s + 1].at[pl.ds(pl.multiple_of(to * nxt, nxt), nxt), :], b["in"][s + 1].at[k], dev)
            for k, (to, dev) in enumerate(devices(part, s + 1))]

    def gather(i, s):
        part, block, h = PARTS[i]
        at = tuple(index(grp) for grp in part[:s + 1]) + (slice(None),) * (len(part) - s)
        piece = tables[block][2].at[(*at, pl.ds(h * WIDTH, WIDTH))]
        sent[i]["ag"] = [send(piece, piece, dev) for _, dev in devices(part, s)]

    def project(i):
        block = PARTS[i][1]
        if block not in ready:
            ready.add(block)
            return
        n = tables[block][2][...].reshape(PART, TRAITS)
        v = jnp.dot(g[:, pl.ds(block * PART, PART)], n, preferred_element_type=F32)
        if not projected:
            p[...] = v
        else:
            p[...] += v
        projected.append(block)

    ready = set()
    projected = []
    for turn, (i, step) in enumerate(ORDER):
        stages = len(PARTS[i][0])
        if step == 0:
            first_send(i)
        elif step <= stages:
            if turn and wide_send:
                wait(wide_send)
                v = wide[0]
                for k in range(7):
                    v = v + wide_in[k]
                wide[1] = v * (1.0 / GROUPS)
                wide_send.clear()
            reduce(i, step - 1)
        else:
            wait(sent[i]["ag"])
            s = 2 * stages - step - 1
            if s >= 0:
                gather(i, s)
            else:
                project(i)
        if turn == 0:
            wait(c_plane)
            v = mean[PLANE][...]
            for k in range(7):
                v = v + mean_in[PLANE][k]
            wide[0] = v
            wide_send = [send(wide.at[0], wide_in.at[k], dev) for k, (_, dev) in enumerate(along)]

    own = jnp.sum(p[...], axis=0, keepdims=True) * (1.0 / ROWS)
    lines = [own[:, :128], own[:, 128:]]
    for h in range(2):
        norm = norms[h][0]
        for v in norms[h][1:]:
            norm = norm + v
        lines.append(norm)
    tile[0] = jnp.concatenate(lines, axis=0)

    def rows_at(c, h):
        return pl.ds(pl.multiple_of(c * 256 + h * 128, 128), 128)

    halves = (1 - me["h"], me["h"])
    c1 = []
    for j, h in enumerate(halves):
        pb[j] = p[rows_at(1 - core, h), :] - own
        c1.append(send(pb.at[j], pb_in.at[j], other_core))
    c1.append(send(tile.at[0], tile_in.at[0], other_core))
    wait(c1[:1])
    hb[...] = (p[rows_at(core, halves[0]), :] - own + pb_in[0]).astype(BF16)
    c2 = [send(hb, hb_in, other_half)]
    wait(c1[1:])
    tile[1] = tile[0] + tile_in[0]
    c2.append(send(tile.at[1], tile_in.at[1], other_half))
    near = p[rows_at(core, halves[1]), :] - own + pb_in[1]
    wait(c2[:1])
    mine = near + hb_in[...].astype(F32)
    full[core, me["h"]] = mine
    c3 = [send(full.at[core, me["h"]], full.at[core, me["h"]], other_half)]

    for c in (1 - core, core):
        cols = full[core, me["h"], :, pl.ds(pl.multiple_of(c * 128, 128), 128)]
        gt[c] = dot_rows(cols, mine).reshape(16, 8, TRAITS)
        if c is not core:
            g1 = [send(gt.at[c], gc_in, other_core)]
    wait(c2[1:])
    tile[2] = tile[1] + tile_in[1]
    spot = index(PLANE)
    every[me["z"], spot] = tile[2]
    m1 = [send(every.at[me["z"], spot], every.at[me["z"], spot], dev) for _, dev in plane]
    wait(g1)
    gc_in[...] = gc_in[...] + gt[core]
    g2 = [send(gc_in.at[to], gh_in.at[k], dev) for k, (to, dev) in enumerate(layer)]
    wait(m1)
    m2 = [send(every.at[me["z"]], every.at[me["z"]], dev) for _, dev in along]
    wait(g2)
    mid = index(("x", "y", "h"))
    v = gc_in[mid]
    for k in range(15):
        v = v + gh_in[k]
    gz[...] = v
    g3 = [send(gz, gz_in.at[k], dev) for k, (_, dev) in enumerate(along)]
    wait(g3)
    v = gz[...]
    for k in range(7):
        v = v + gz_in[k]
    gall[core, mid] = v
    piece = gall.at[core, mid]
    g4 = [send(piece, piece, dev) for _, dev in layer]
    wait(c3)
    c4 = [send(full.at[core], full.at[core], other_core)]
    wait(c4)
    proj_copy = pltpu.make_async_copy(full, proj_hbm, load_sem.at[0])
    proj_copy.start()
    wait(g4)
    g5 = [send(gall.at[core], gall.at[core], other_core)]
    wait(m2)
    means = jnp.concatenate([every[:, :, r, :].reshape(GROUPS, 128) for r in range(2)], axis=1)
    norm = jnp.concatenate(
        [jnp.sum(every[:, :, r, :].reshape(GROUPS, 128), axis=0, keepdims=True) for r in (2, 3)], axis=1)
    centre = jnp.sum(means, axis=0, keepdims=True) * (1.0 / GROUPS)
    gap = means - centre
    between = dot_rows(gap, gap) * float(ROWS)
    off = jnp.concatenate([tile[2, 0:1], tile[2, 1:2]], axis=1) - centre
    stat_ref[...] = jnp.concatenate([norm, off, jnp.zeros((6, TRAITS), F32)], axis=0)
    wait(g5)
    gram_ref[...] = gall[...].reshape(TRAITS, TRAITS) + between
    for cp in started:
        cp.wait_send()
    proj_copy.wait()
    assert count[0] == COPIES, count[0]


COPIES = 74 + 7 * any(part[0] == ALONG for part in BLOCKS) + sum(
    size_of(part[0]) - 1 + 4 * sum(size_of(grp) - 1 for grp in part) for part in BLOCKS)


def scratch_of():
    vmem = pltpu.VMEM
    shapes = [vmem((ROWS, SNPS), BF16), vmem((ROWS, TRAITS), BF16), vmem((SNPS, TRAITS), F32), vmem((SNPS, 128), F32)]
    for _ in range(2):
        shapes += [vmem((1, TRAITS), F32), vmem((7, 1, TRAITS), F32)]
    shapes += [vmem((2, 1, TRAITS), F32), vmem((7, 1, TRAITS), F32)]
    for part in BLOCKS:
        sizes = [size_of(grp) for grp in part]
        shapes += [vmem((sizes[0], 8, 128), F32), vmem((sizes[0] - 1, 8, 128), F32), vmem((*sizes, OWN, TRAITS), BF16)]
    for part, _, _ in PARTS:
        sizes = [size_of(grp) for grp in part]
        blk, n = [], PART
        for s in sizes:
            n //= s
            blk.append(n)
        shapes += [vmem((sizes[0] - 1, blk[0], WIDTH), BF16), vmem((blk[0], WIDTH), F32)]
        shapes += [vmem((s - 1, b, WIDTH), BF16) for s, b in zip(sizes, blk)]
        shapes += [vmem((b, WIDTH), F32) for b in blk[:-1]]
        shapes += [vmem((b, WIDTH), BF16) for b in blk[:-1]]
    shapes += [
        vmem((ROWS, TRAITS), F32), vmem((2, 128, TRAITS), F32), vmem((2, 128, TRAITS), F32),
        vmem((128, TRAITS), BF16), vmem((128, TRAITS), BF16), vmem((2, 2, 128, TRAITS), F32),
        vmem((3, 4, 128), F32), vmem((2, 4, 128), F32), vmem((8, 8, 4, 128), F32),
        vmem((2, 16, 8, TRAITS), F32), vmem((16, 8, TRAITS), F32), vmem((15, 8, TRAITS), F32), vmem((8, TRAITS), F32),
        vmem((7, 8, TRAITS), F32), vmem((2, 16, 8, TRAITS), F32),
        pltpu.SemaphoreType.DMA((5,)), pltpu.SemaphoreType.DMA((COPIES,)), pltpu.SemaphoreType.DMA((COPIES,)),
    ]
    return shapes


def finish(gram_ref, stat_ref, proj_ref, basis_ref, fit_ref, cov_ref, score_ref):
    gram = gram_ref[...]
    norm_row, off = stat_ref[0:1, :], stat_ref[1:2, :]
    square = (TRAITS, TRAITS)
    eye = lax.broadcasted_iota(jnp.int32, square, 0) == lax.broadcasted_iota(jnp.int32, square, 1)
    diag_row = jnp.sum(jnp.where(eye, gram, 0.0), axis=0, keepdims=True)
    step_row = norm_row / (diag_row + (SAMPLES / 8.0) * norm_row)
    step_col = jnp.sum(jnp.where(eye, jnp.broadcast_to(step_row, square), 0.0), axis=1, keepdims=True)
    cov = step_col * gram * step_row * (1.0 / SAMPLES)
    cov_ref[...] = cov
    spread = jnp.sum(step_row * step_row * diag_row, axis=1, keepdims=True) * (1.0 / SAMPLES) + 1e-6
    dims1 = (((1,), (1,)), ((), ()))
    loading = lax.dot_general(basis_ref[...], cov, (((1,), (1,)), ((), ())), precision=HIGHEST,
                              preferred_element_type=F32) * (TRAITS / spread)
    high = loading.astype(BF16)
    low = (loading - high.astype(F32)).astype(BF16)
    f = ((proj_ref[...].reshape(ROWS, TRAITS) + off) * step_row).astype(BF16)
    fit_ref[...] = f
    score_ref[...] = (lax.dot_general(high, f, dims1, preferred_element_type=F32)
                      + lax.dot_general(low, f, dims1, preferred_element_type=F32))


def local(genotypes, traits, trait_basis):
    anywhere = pl.BlockSpec(memory_space=pl.ANY)
    inside = pl.BlockSpec(memory_space=pltpu.VMEM)
    gram, stat, proj = pl.pallas_call(
        kernel,
        out_shape=(
            jax.ShapeDtypeStruct((TRAITS, TRAITS), F32),
            jax.ShapeDtypeStruct((8, TRAITS), F32),
            jax.ShapeDtypeStruct((2, 2, 128, TRAITS), F32),
        ),
        in_specs=[anywhere, anywhere],
        out_specs=(inside, inside, anywhere),
        scratch_shapes=scratch_of(),
        compiler_params=pltpu.CompilerParams(
            collective_id=0, has_side_effects=True, vmem_limit_bytes=56 * 2**20),
    )(genotypes, traits)
    fitted, covariance, scores = pl.pallas_call(
        finish,
        out_shape=(
            jax.ShapeDtypeStruct((ROWS, TRAITS), BF16),
            jax.ShapeDtypeStruct((TRAITS, TRAITS), F32),
            jax.ShapeDtypeStruct((RANK, ROWS), F32),
        ),
        in_specs=[inside] * 4,
        out_specs=(inside, inside, inside),
    )(gram, stat, proj, trait_basis.T)
    return fitted, covariance, scores.T


def solution(mesh):
    return jax.shard_map(
        local,
        mesh=mesh,
        in_specs=(P("samp", "snp"), P("samp", None), P()),
        out_specs=(P("samp", None), P(), P("samp", None)),
        check_vma=False,
    )
```
